32 devices in a mesh: runs: 2 (over y), gx: 4 (over z), gy: 2 (over x), gz: 2 (over core).
Axes of the slice: x: 2, y: 2, z: 4, core: 2. Of those that a mesh axis runs over, the one named last changes fastest.
Arguments:
- offsets: float32 [3, 32768], P(None, ('runs', 'gx', 'gy', 'gz')), parts along dimension 1, may hold values from -0.5 to 0.5
- particle_mass: float32 [32768], P(('runs', 'gx', 'gy', 'gz')), parts along dimension 0, may hold values from 0.5 to 2
- velocity: float32 [3, 32768], P(None, ('runs', 'gx', 'gy', 'gz')), parts along dimension 1, may hold values from -6 to 6
- home_cell: int32 [32768], P(('runs', 'gx', 'gy', 'gz')), parts along dimension 0, may hold values from 0 to 4095
- home_tile: int32 [32768], P(('runs', 'gx', 'gy', 'gz')), parts along dimension 0, may hold values from 0 to 7, as said below
- conv1_weight: bfloat16 [16, 4, 3, 3, 3], replicated, may hold values from -2.5 to 2.5
- conv1_bias: float32 [16], replicated, may hold values from -3 to 3
- conv2_weight: bfloat16 [16, 16, 3, 3, 3], replicated, may hold values from -0.3125 to 0.3125
- conv2_bias: float32 [16], replicated, may hold values from -3 to 3
- head_weight: bfloat16 [3, 16], replicated, may hold values from -1.5 to 1.5
Outputs:
- forces: float32 [3, 32768], P(None, ('runs', 'gx', 'gy', 'gz')), parts along dimension 1
The draws below stay inside these ranges and needn't reach their ends.
There are 2 independent parts, one for each index of `runs`. The reference program is written for one: setup_inputs(seed, part) draws one part's arguments, and reference() takes and returns one part's arrays. A program takes and returns all parts, laid end to end along the dimension named above; an argument that names none is the same for every part. Nothing has to cross between parts.
Inputs may be any that keep to these rules, and one draw needn't show every extreme that they name: `home_tile`: within the rows of one device (aligned blocks of 1024 rows) no tile is named more than 256 times; in every draw one tile is named exactly 256 times in every block.
All inputs are finite; a program needn't handle non-finite values.
Results may differ from the reference program's by a relative error of at most 0.0057.
Values may be sent and summed in bfloat16 or wider, within the bound.
No kernel may reach another device: no remote copies, remote signals or barrier semaphores. Data moves between devices by JAX's collectives and lax.ppermute only.
A program may use at most 64 MiB of HBM per device.

```python
import math
import jax
import jax.numpy as jnp
from jax import lax

CH = 16
PAINTED = 4
TX = 16
TY = 128
TZ = 2
PDEV = 1024
NTILE = 8
TILE_COLS = 2
LEVELS = 2
CAP = 256
NX = 64
NY = 256
NZ = 4
PARTICLES = 16384


def draw_home_tile(key, part):
    block_rows = PARTICLES // PDEV
    hot_tile = jax.random.randint(jax.random.fold_in(key, 7), (), 0, NTILE).astype(jnp.int32)
    block_keys = jax.random.split(jax.random.fold_in(key, 11), block_rows)

    def one_block(block_key):
        key_pick, key_order = jax.random.split(block_key)
        chosen = jax.random.permutation(key_pick, (NTILE - 1) * CAP)[:PDEV - CAP].astype(jnp.int32)
        spread = chosen // CAP
        spread = spread + (spread >= hot_tile).astype(jnp.int32)
        gathered = jnp.concatenate([jnp.zeros((CAP,), jnp.int32) + hot_tile, spread])
        return gathered[jax.random.permutation(key_order, PDEV)]
    return jax.vmap(one_block)(block_keys).reshape(-1).astype(jnp.int32)


def set_ends(values, stream_key, low, largest):
    longest = values.shape.index(max(values.shape))
    spots = []
    for shift in (0, 1):
        where = [jax.random.randint(jax.random.fold_in(stream_key, axis), (), 0, length) for axis, length in enumerate(values.shape)]
        where[longest] = (where[longest] + shift) % values.shape[longest]
        spots.append(tuple(where))
    return values.at[spots[0]].set(low).at[spots[1]].set(largest)


def block_levels(rng, shape, cuts, smallest, high):
    def one(dim, parts):
        steps = jax.random.uniform(jax.random.fold_in(jax.random.fold_in(rng, 6), dim), (parts,), jnp.float32, smallest / len(cuts), high / len(cuts))
        return jnp.repeat(jnp.exp(steps), shape[dim] // parts).reshape((-1,) + (1,) * (len(shape) - dim - 1))

    factor_of = one(*cuts[0])
    for cut in cuts[1:]:
        factor_of = factor_of * one(*cut)
    return factor_of


def normal_values(stream_key, dims, deviation, limit, shards=(), kind=jnp.bfloat16):
    array = jax.random.normal(stream_key, dims, jnp.float32) * deviation
    if len(shards) > 0:
        array = block_levels(stream_key, dims, shards, -0.22, 0.18) * array
    return jnp.clip(array, min=-limit, max=limit).astype(kind)


def setup_inputs(seed: int = 0, part: int = 0) -> dict:
    keys = jax.random.split(jax.random.key(seed), 11)
    part_splits = jax.random.split(jax.random.fold_in(keys[10], part), 11)
    offsets = jnp.clip(jax.random.uniform(part_splits[0], (3, PARTICLES), jnp.float32, -0.5, 0.5) * block_levels(part_splits[0], (3, PARTICLES), ((1, 16),), -0.4, 0.0), -0.5, 0.5)
    particle_mass = jnp.clip(jnp.exp(math.log(2.0) - 1.3862944 * jax.random.uniform(part_splits[1], (PARTICLES,), jnp.float32) ** block_levels(part_splits[1], (PARTICLES,), ((0, 16),), -0.2, 0.2)), 0.5, 2.0)
    velocity = normal_values(part_splits[2], (3, PARTICLES), 1.0, 6.0, ((1, 16),), jnp.float32)
    home_cell = set_ends(jax.random.randint(part_splits[3], (PARTICLES,), 0, TZ * TX * TY), jax.random.fold_in(part_splits[3], 1), 0, (TZ * TX * TY) - 1).astype(jnp.int32)
    home_tile = draw_home_tile(jax.random.fold_in(jax.random.fold_in(keys[10], part), 71), part)
    conv1_weight = normal_values(keys[5], (CH, PAINTED, 3, 3, 3), 6 ** -0.5, 2.5)
    conv1_bias = normal_values(keys[6], (CH,), 0.5, 3.0, (), jnp.float32)
    conv2_weight = normal_values(keys[7], (CH, CH, 3, 3, 3), (27 * CH) ** -0.5, 0.3125)
    conv2_bias = normal_values(keys[8], (CH,), 0.5, 3.0, (), jnp.float32)
    head_weight = normal_values(keys[9], (3, CH), CH ** -0.5, 1.5)
    return dict(offsets=offsets, particle_mass=particle_mass, velocity=velocity, home_cell=home_cell, home_tile=home_tile, conv1_weight=conv1_weight, conv1_bias=conv1_bias, conv2_weight=conv2_weight, conv2_bias=conv2_bias, head_weight=head_weight)


def particle_cells(home_cell, home_tile):
    total_rows = home_cell.shape[0]
    holder = jnp.arange(total_rows, dtype=jnp.int32) // PDEV
    plane_group = holder % LEVELS
    tile_row = home_tile // TILE_COLS
    tile_column = home_tile % TILE_COLS
    local_z = home_cell // (TX * TY)
    local_x = (home_cell // TY) % TX
    local_y = home_cell % TY
    return (plane_group * TZ + local_z, tile_row * TX + local_x, tile_column * TY + local_y)


def axis_pair(base, fraction):
    step_dir = jnp.where(fraction >= 0.0, 1, -1).astype(jnp.int32)
    return (base, base + step_dir), (1.0 - jnp.abs(fraction), jnp.abs(fraction))


def corner_list(positions, offsets):
    z_pair, z_weight = axis_pair(positions[0], offsets[0])
    x_pair, x_weight = axis_pair(positions[1], offsets[1])
    y_pair, y_weight = axis_pair(positions[2], offsets[2])
    result = []
    for pick_z in range(2):
        for pick_x in range(2):
            for pick_y in range(2):
                plane_at = z_pair[pick_z]
                inside = ((plane_at >= 0) & (plane_at < NZ)).astype(jnp.float32)
                weight = z_weight[pick_z] * x_weight[pick_x] * y_weight[pick_y] * inside
                flat_index = (jnp.clip(plane_at, 0, NZ - 1) * NX + x_pair[pick_x] % NX) * NY + y_pair[pick_y] % NY
                result.append((flat_index.astype(jnp.int32), weight))
    return result


def convolve_all(mesh_field, weight, bias_vec, head_weight):
    padded = jnp.pad(mesh_field, ((0, 0), (1, 1), (0, 0), (0, 0)))
    padded = jnp.pad(padded, ((0, 0), (0, 0), (1, 1), (1, 1)), mode="wrap")

    def one_plane(plane_index):
        slab_part = lax.dynamic_slice_in_dim(padded, plane_index, 3, 1).astype(jnp.float32)
        summed = lax.conv_general_dilated(slab_part[None], weight.astype(jnp.float32), (1, 1, 1), "VALID", dimension_numbers=("NCDHW", "OIDHW", "NCDHW"), precision=lax.Precision.HIGHEST)[0, :, 0]
        output = jax.nn.silu(summed + bias_vec[:, None, None]).astype(jnp.bfloat16)
        if head_weight is None:
            return output
        widened = lax.optimization_barrier(output).astype(jnp.float32)
        return jnp.einsum("oc,cxy->oxy", head_weight.astype(jnp.float32), widened, precision=lax.Precision.HIGHEST)

    planes = lax.map(one_plane, jnp.arange(NZ, dtype=jnp.int32))
    return jnp.transpose(planes, (1, 0, 2, 3))


def reference(offsets, particle_mass, velocity, home_cell, home_tile, conv1_weight, conv1_bias, conv2_weight, conv2_bias, head_weight):
    positions = particle_cells(home_cell, home_tile)
    corners = corner_list(positions, offsets)
    values = jnp.concatenate([particle_mass[None], particle_mass[None] * velocity], axis=0)
    mesh_grid = jnp.zeros((PAINTED, NZ * NX * NY), jnp.float32)
    for flat_index, weight in corners:
        mesh_grid = mesh_grid.at[:, flat_index].add(values * weight[None])
    density = mesh_grid.reshape(PAINTED, NZ, NX, NY).astype(jnp.bfloat16)
    hidden = convolve_all(density, conv1_weight, conv1_bias, None)
    force_field = convolve_all(hidden, conv2_weight, conv2_bias, head_weight).reshape(3, NZ * NX * NY)
    forces = jnp.zeros((3, offsets.shape[1]), jnp.float32)
    for flat_index, weight in corners:
        forces = forces + force_field[:, flat_index] * weight[None]
    return forces
```

```python
import functools
import jax
import jax.numpy as jnp
from jax import lax
from jax.experimental import pallas as pl
from jax.experimental.pallas import tpu as pltpu
from jax.sharding import PartitionSpec as P

TX = 16
TY = 128
TZ = 2
SEGMENT = 256
F32 = jnp.float32
BF16 = jnp.bfloat16
VMEM_SPEC = pl.BlockSpec(memory_space=pltpu.VMEM)
SMEM_SPEC = pl.BlockSpec(memory_space=pltpu.SMEM)


def exchange_pairs(count, step):
    if count & (count - 1) == 0:
        return [(i, i ^ step) for i in range(count)]
    return [(i, (i + step) % count) for i in range(count)]


def return_pairs(count, step):
    return [(target, source) for source, target in exchange_pairs(count, step)]


def rows_iota(rows, lanes):
    return lax.broadcasted_iota(jnp.int32, (rows, lanes), 0).astype(F32)


def hat(distance):
    return jnp.maximum(1.0 - jnp.abs(distance), 0.0)


def wrapped_x(px, x_start, nx):
    rel = px - x_start
    rel = jnp.where(rel < -1.0, rel + nx, rel)
    return jnp.where(rel > nx - 1.0, rel - nx, rel)


def write_y_weights(py, ny, high_ref, low_ref):
    lanes = py.shape[1]
    base = jnp.floor(py + 0.5)
    frac = py - base
    near = base + jnp.where(frac >= 0.0, 1.0, -1.0)
    base = jnp.where(base >= ny, base - ny, base)
    near = jnp.where(near < 0.0, near + ny, near)
    near = jnp.where(near >= ny, near - ny, near)
    w_near = jnp.abs(frac)
    w_base = 1.0 - w_near

    def tiled(row):
        return jnp.broadcast_to(row, (16, lanes)).astype(BF16)

    bh, nh = tiled(w_base), tiled(w_near)
    if low_ref is not None:
        bl = (jnp.broadcast_to(w_base, (16, lanes)) - bh.astype(F32)).astype(BF16)
        nl = (jnp.broadcast_to(w_near, (16, lanes)) - nh.astype(F32)).astype(BF16)
    index = lax.broadcasted_iota(jnp.int32, (16, lanes), 0).astype(F32).astype(BF16)
    zero = jnp.zeros((16, lanes), BF16)
    for start in range(0, ny, SEGMENT):
        length = min(SEGMENT, ny - start)
        at_base = tiled(jnp.clip(base - start, -1.0, SEGMENT))
        at_near = tiled(jnp.clip(near - start, -1.0, SEGMENT))
        for row in range(0, length, 16):
            here = index + jnp.asarray(row, BF16)
            on_base, on_near = here == at_base, here == at_near
            rows = pl.ds(start + row, 16)
            high_ref[rows, :] = jnp.where(on_base, bh, jnp.where(on_near, nh, zero))
            if low_ref is not None:
                low_ref[rows, :] = jnp.where(on_base, bl, jnp.where(on_near, nl, zero))


def paint_kernel(nz, nx, ny, counts, first, *refs):
    place = refs[0]
    sources = refs[1 : 1 + len(counts)]
    refs = refs[1 + len(counts) :]
    if not first:
        before, refs = refs[0], refs[1:]
    outs, (rows_ref, a_ref, wh_ref, wl_ref, acc) = refs[:-5], refs[-5:]
    ext = TX + 4
    per_x = nz * 4
    half = ext * per_x
    total = 0
    for source, count in zip(sources, counts):
        for index in range(count):
            rows_ref[total] = source[pl.ds(8 * index, 8), :]
            total += 1
    x_start = place[0]
    if first:
        acc[...] = jnp.zeros_like(acc)
    else:
        acc[...] = before[...]

    def one_block(index, carry):
        rows = rows_ref[index]
        lanes = rows.shape[1]
        write_y_weights(rows[2:3], ny, wh_ref, wl_ref)
        rel = wrapped_x(rows[1:2], x_start, nx)
        wx = hat(rows_iota(24, lanes) - rel)
        plane = lax.broadcasted_iota(jnp.int32, (per_x, lanes), 0)
        wz = hat((plane // 4).astype(F32) - rows[0:1])
        channel = plane % 4
        value = jnp.where(
            channel == 0,
            rows[3:4],
            jnp.where(channel == 1, rows[4:5], jnp.where(channel == 2, rows[5:6], rows[6:7])),
        )
        spread = wz * value
        for x in range(ext):
            full = spread * wx[x : x + 1]
            high = full.astype(BF16)
            a_ref[pl.ds(x * per_x, per_x), :] = high
            a_ref[pl.ds(half + x * per_x, per_x), :] = (full - high.astype(F32)).astype(BF16)
        dims = (((1,), (1,)), ((), ()))
        main = lax.dot_general(a_ref[...], wh_ref[...], dims, preferred_element_type=F32)
        side = lax.dot_general(
            a_ref[pl.ds(0, half), :], wl_ref[...], dims, preferred_element_type=F32
        )
        acc[...] += main[:half] + main[half:] + side
        return carry

    lax.fori_loop(0, total, one_block, 0)
    if len(outs) == 1:
        outs[0][...] = acc[...]
    else:
        keep, send = outs
        width = keep.shape[0]
        sub = TX * per_x // 2
        level = place[1].astype(jnp.int32)
        keep[...] = acc[pl.ds(pl.multiple_of(level * sub, sub), width), :]
        send[...] = acc[pl.ds(pl.multiple_of((1 - level) * sub, sub), width), :]


def paint(place, sources, before, nz, nx, ny, split):
    counts = [source.shape[0] // 8 for source in sources]
    lanes = sources[0].shape[1]
    per_x = nz * 4
    half = (TX + 4) * per_x
    if split:
        shape = jax.ShapeDtypeStruct(((TX // 2 + 4) * per_x, ny), F32)
        out_shape = (shape, shape)
        out_specs = (VMEM_SPEC, VMEM_SPEC)
    else:
        out_shape = jax.ShapeDtypeStruct((half, ny), F32)
        out_specs = VMEM_SPEC
    args = [place] + list(sources) + ([] if before is None else [before])
    return pl.pallas_call(
        functools.partial(paint_kernel, nz, nx, ny, counts, before is None),
        out_shape=out_shape,
        in_specs=[SMEM_SPEC] + [VMEM_SPEC] * (len(args) - 1),
        out_specs=out_specs,
        scratch_shapes=[
            pltpu.VMEM((sum(counts), 8, lanes), F32),
            pltpu.VMEM((2 * half, lanes), BF16),
            pltpu.VMEM((ny, lanes), BF16),
            pltpu.VMEM((ny, lanes), BF16),
            pltpu.VMEM((half, ny), F32),
        ],
        cost_estimate=pl.CostEstimate(
            flops=6 * half * lanes * ny * sum(counts),
            bytes_accessed=4 * half * ny,
            transcendentals=0,
        ),
        name="paint",
    )(*args)


def prepare_kernel(nz, w1_ref, w2_ref, b1_ref, b2_ref, hw_ref, o1, o2, ob1, ob2, oh, t1, t2):
    per_in = nz * 4
    per_mid = nz * 16
    t1[...] = jnp.zeros_like(t1)
    t2[...] = jnp.zeros_like(t2)
    oh[...] = jnp.zeros_like(oh)

    def at(a, b, e):
        return (a * 3 + b) * 3 + e

    for b in range(3):
        for e in range(3):
            for q in range(2):
                xi = q + b
                for zo in range(nz):
                    for a in range(3):
                        zi = zo + a - 1
                        if zi < 0 or zi >= nz:
                            continue
                        t1[
                            pl.ds((e * 4 + xi) * per_in + zi * 4, 4),
                            pl.ds((q * nz + zo) * 16, 16),
                        ] = w1_ref[at(a, b, e)].astype(F32)
                        t2[
                            pl.ds(((e * 2 + q) * nz + zo) * 16, 16),
                            pl.ds((xi * nz + zi) * 16, 16),
                        ] = w2_ref[at(a, b, e)].astype(F32)
    o1[...] = t1[...].T.astype(BF16)
    o2[...] = t2[...].astype(BF16)
    for q in range(2 * nz):
        oh[pl.ds(q * 4, 3), pl.ds(q * 16, 16)] = hw_ref[...].astype(F32)
    for source, target in ((b1_ref, ob1), (b2_ref, ob2)):
        shape = (2 * per_mid, 16)
        pick = lax.broadcasted_iota(jnp.int32, shape, 0) % 16 == lax.broadcasted_iota(
            jnp.int32, shape, 1
        )
        target[...] = jnp.sum(
            jnp.where(pick, jnp.broadcast_to(source[...], shape), 0.0), axis=1, keepdims=True
        )


def prepare(conv1_weight, conv1_bias, conv2_weight, conv2_bias, head_weight, nz):
    w1 = jnp.transpose(conv1_weight, (2, 3, 4, 1, 0)).reshape(27, 4, 16)
    w2 = jnp.transpose(conv2_weight, (2, 3, 4, 0, 1)).reshape(27, 16, 16)
    rows = 2 * nz * 16
    return pl.pallas_call(
        functools.partial(prepare_kernel, nz),
        out_shape=(
            jax.ShapeDtypeStruct((rows, 3 * 4 * nz * 4), BF16),
            jax.ShapeDtypeStruct((3 * rows, 4 * nz * 16), BF16),
            jax.ShapeDtypeStruct((rows, 1), F32),
            jax.ShapeDtypeStruct((rows, 1), F32),
            jax.ShapeDtypeStruct((2 * nz * 4, rows), F32),
        ),
        in_specs=[VMEM_SPEC] * 5,
        out_specs=(VMEM_SPEC,) * 5,
        scratch_shapes=[
            pltpu.VMEM((3 * 4 * nz * 4, rows), F32),
            pltpu.VMEM((3 * rows, 4 * nz * 16), F32),
        ],
        cost_estimate=pl.CostEstimate(flops=1000000, bytes_accessed=1000000, transcendentals=0),
        name="prepare",
    )(w1, w2, conv1_bias[None], conv2_bias[None], head_weight)


def silu(v):
    return v / (1.0 + jnp.exp(-v))


def mesh_kernel(nz, keep, got, w1, w2, b1, b2, hw, out, d3, hid):
    per_in = nz * 4
    per_mid = nz * 16
    ny = keep.shape[1]
    width = keep.shape[0] // per_in
    density = (keep[...] + got[...]).astype(BF16)
    wide = density.astype(F32)
    d3[0] = pltpu.roll(wide, 1, 1).astype(BF16)
    d3[1] = density
    d3[2] = pltpu.roll(wide, ny - 1, 1).astype(BF16)
    for x in range(0, width - 2, 2):
        window = pl.ds(x * per_in, 4 * per_in)
        taps = jnp.concatenate([d3[0, window, :], d3[1, window, :], d3[2, window, :]], axis=0)
        summed = jnp.dot(w1[...], taps, preferred_element_type=F32)
        hid[pl.ds(x * per_mid, 2 * per_mid), :] = silu(summed + b1[...]).astype(BF16)
    head = hw[...].astype(BF16)
    rows = 2 * per_mid
    for x in range(0, width - 4, 2):
        parts = jnp.dot(
            w2[...], hid[pl.ds(x * per_mid, 4 * per_mid), :], preferred_element_type=F32
        )
        summed = (
            pltpu.roll(parts[:rows], 1, 1)
            + parts[rows : 2 * rows]
            + pltpu.roll(parts[2 * rows :], ny - 1, 1)
        )
        features = silu(summed + b2[...]).astype(BF16)
        out[pl.ds(x * per_in, 2 * per_in), :] = jnp.dot(
            head, features, preferred_element_type=F32
        )


def mesh_step(keep, got, weights, nz):
    per_in = nz * 4
    ny = keep.shape[1]
    width = keep.shape[0] // per_in
    return pl.pallas_call(
        functools.partial(mesh_kernel, nz),
        out_shape=jax.ShapeDtypeStruct(((width - 4) * per_in, ny), F32),
        in_specs=[VMEM_SPEC] * 7,
        out_specs=VMEM_SPEC,
        scratch_shapes=[
            pltpu.VMEM((3, keep.shape[0], ny), BF16),
            pltpu.VMEM(((width - 2) * nz * 16, ny), BF16),
        ],
        name="mesh_step",
    )(keep, got, *weights)


def sample_kernel(nz, nx, ny, place, own, other, *refs):
    count = (len(refs) - 3) // 2
    sources, outs = refs[:count], refs[count : 2 * count]
    f_ref, wh_ref, t_ref = refs[2 * count :]
    per_x = nz * 4
    span = own.shape[0]
    half = 2 * span
    for index, source in enumerate((own, other)):
        full = source[...]
        high = full.astype(BF16)
        f_ref[pl.ds(index * span, span), :] = high
        f_ref[pl.ds(half + index * span, span), :] = (full - high.astype(F32)).astype(BF16)
    x_start = place[0] + 2.0
    level = place[1]
    width = span // per_x
    for source, out in zip(sources, outs):
        lanes = source.shape[1]
        write_y_weights(source[2:3, :], ny, wh_ref, None)
        t_ref[...] = jnp.dot(f_ref[...], wh_ref[...], preferred_element_type=F32)
        rel = wrapped_x(source[1:2, :], x_start, nx)
        total = jnp.zeros((per_x, lanes), F32)
        for index, offset in enumerate((level * width, (1.0 - level) * width)):
            wx = hat(rows_iota(8 * ((width + 7) // 8), lanes) + (offset - rel))
            for x in range(width):
                row = index * span + x * per_x
                total += wx[x : x + 1] * (
                    t_ref[pl.ds(row, per_x), :] + t_ref[pl.ds(half + row, per_x), :]
                )
        plane = lax.broadcasted_iota(jnp.int32, (per_x, lanes), 0)
        total = total * hat((plane // 4).astype(F32) - source[0:1, :])
        summed = total[0:4]
        for z in range(1, nz):
            summed = summed + total[z * 4 : z * 4 + 4]
        out[...] = summed


def sample(place, own, other, sources, nz, nx, ny):
    lanes = sources[0].shape[1]
    span = own.shape[0]
    return pl.pallas_call(
        functools.partial(sample_kernel, nz, nx, ny),
        out_shape=tuple(jax.ShapeDtypeStruct((4, lanes), F32) for _ in sources),
        in_specs=[SMEM_SPEC] + [VMEM_SPEC] * (2 + len(sources)),
        out_specs=tuple(VMEM_SPEC for _ in sources),
        scratch_shapes=[
            pltpu.VMEM((4 * span, ny), BF16),
            pltpu.VMEM((ny, lanes), BF16),
            pltpu.VMEM((4 * span, lanes), F32),
        ],
        cost_estimate=pl.CostEstimate(
            flops=8 * span * lanes * ny * len(sources),
            bytes_accessed=8 * span * ny,
            transcendentals=0,
        ),
        name="sample",
    )(place, own, other, *sources)


def on_device(
    offsets,
    particle_mass,
    velocity,
    home_cell,
    home_tile,
    conv1_weight,
    conv1_bias,
    conv2_weight,
    conv2_bias,
    head_weight,
):
    columns = lax.axis_size("gy")
    rows = lax.axis_size("gx")
    levels = lax.axis_size("gz")
    assert levels == 2
    nz, nx, ny = TZ * levels, TX * rows, TY * columns
    level = lax.axis_index("gz")
    base_z = home_cell // (TX * TY) + level * TZ
    base_x = home_tile // columns * TX + home_cell // TY % TX
    base_y = home_tile % columns * TY + home_cell % TY
    base = jnp.stack([base_z, base_x, base_y]).astype(F32)
    block = jnp.concatenate(
        [
            base + offsets,
            particle_mass[None],
            particle_mass[None] * velocity,
            jnp.zeros_like(particle_mass)[None],
        ],
        axis=0,
    )
    place = jnp.stack([lax.axis_index("gx") * TX - 2, level]).astype(F32)
    line = jnp.concatenate(
        [block]
        + [lax.ppermute(block, "gy", exchange_pairs(columns, s)) for s in range(1, columns)],
        axis=0,
    )
    arrived = [lax.ppermute(line, "gx", exchange_pairs(rows, s)) for s in range(1, rows)]
    weights = prepare(conv1_weight, conv1_bias, conv2_weight, conv2_bias, head_weight, nz)
    early = paint(place, [line], None, nz, nx, ny, False)
    keep, send = paint(place, arrived, early, nz, nx, ny, True)
    got = lax.ppermute(send, "gz", exchange_pairs(levels, 1))
    own = mesh_step(keep, got, weights, nz)
    other = lax.ppermute(own, "gz", exchange_pairs(levels, 1))
    away = sample(place, own, other, [part[:8] for part in arrived], nz, nx, ny)
    home = [
        lax.ppermute(part, "gx", return_pairs(rows, s)) for s, part in enumerate(away, start=1)
    ]
    (here,) = sample(place, own, other, [block], nz, nx, ny)
    for part in home:
        here = here + part
    return here[:3]


def solution(mesh):
    in_specs = (
        P(None, ("runs", "gx", "gy", "gz")),
        P(("runs", "gx", "gy", "gz")),
        P(None, ("runs", "gx", "gy", "gz")),
        P(("runs", "gx", "gy", "gz")),
        P(("runs", "gx", "gy", "gz")),
        P(),
        P(),
        P(),
        P(),
        P(),
    )
    out_specs = P(None, ("runs", "gx", "gy", "gz"))
    return jax.shard_map(
        on_device, mesh=mesh, in_specs=in_specs, out_specs=out_specs, check_vma=False
    )
```

```python
import functools
import jax
import jax.numpy as jnp
from jax import lax
from jax.experimental import pallas as pl
from jax.experimental.pallas import tpu as pltpu
from jax.sharding import PartitionSpec as P

TX = 16
TY = 128
TZ = 2
SEGMENT = 256
F32 = jnp.float32
BF16 = jnp.bfloat16
VMEM_SPEC = pl.BlockSpec(memory_space=pltpu.VMEM)
SMEM_SPEC = pl.BlockSpec(memory_space=pltpu.SMEM)


def exchange_pairs(count, step):
    if count & (count - 1) == 0:
        return [(i, i ^ step) for i in range(count)]
    return [(i, (i + step) % count) for i in range(count)]


def return_pairs(count, step):
    return [(target, source) for source, target in exchange_pairs(count, step)]


def rows_iota(rows, lanes):
    return lax.broadcasted_iota(jnp.int32, (rows, lanes), 0).astype(F32)


def hat(distance):
    return jnp.maximum(1.0 - jnp.abs(distance), 0.0)


def wrapped_x(px, x_start, nx):
    rel = px - x_start
    rel = jnp.where(rel < -1.0, rel + nx, rel)
    return jnp.where(rel > nx - 1.0, rel - nx, rel)


def write_y_weights(py, ny, high_ref, low_ref):
    lanes = py.shape[1]
    base = jnp.floor(py + 0.5)
    frac = py - base
    near = base + jnp.where(frac >= 0.0, 1.0, -1.0)
    base = jnp.where(base >= ny, base - ny, base)
    near = jnp.where(near < 0.0, near + ny, near)
    near = jnp.where(near >= ny, near - ny, near)
    w_near = jnp.abs(frac)
    w_base = 1.0 - w_near

    def tiled(row):
        return jnp.broadcast_to(row, (16, lanes)).astype(BF16)

    bh, nh = tiled(w_base), tiled(w_near)
    if low_ref is not None:
        bl = (jnp.broadcast_to(w_base, (16, lanes)) - bh.astype(F32)).astype(BF16)
        nl = (jnp.broadcast_to(w_near, (16, lanes)) - nh.astype(F32)).astype(BF16)
    index = lax.broadcasted_iota(jnp.int32, (16, lanes), 0).astype(F32).astype(BF16)
    zero = jnp.zeros((16, lanes), BF16)
    for start in range(0, ny, SEGMENT):
        length = min(SEGMENT, ny - start)
        at_base = tiled(jnp.clip(base - start, -1.0, SEGMENT))
        at_near = tiled(jnp.clip(near - start, -1.0, SEGMENT))
        for row in range(0, length, 16):
            here = index + jnp.asarray(row, BF16)
            on_base, on_near = here == at_base, here == at_near
            rows = pl.ds(start + row, 16)
            high_ref[rows, :] = jnp.where(on_base, bh, jnp.where(on_near, nh, zero))
            if low_ref is not None:
                low_ref[rows, :] = jnp.where(on_base, bl, jnp.where(on_near, nl, zero))


def nbytes(shapes):
    total = 0
    for shape in shapes:
        size = jnp.dtype(shape.dtype).itemsize
        for extent in shape.shape:
            size *= extent
        total += size
    return total


def run_kernel(kernel, name, args, out_shape, scratch, flops=0, smem=1):
    outs = out_shape if isinstance(out_shape, tuple) else (out_shape,)
    moved = nbytes(args) + nbytes(outs)
    grant = moved + nbytes(scratch) + (4 << 20)
    specs = [SMEM_SPEC] * smem + [VMEM_SPEC] * (len(args) - smem)
    return pl.pallas_call(
        kernel,
        out_shape=out_shape,
        in_specs=specs,
        out_specs=tuple(VMEM_SPEC for _ in outs) if isinstance(out_shape, tuple) else VMEM_SPEC,
        scratch_shapes=[pltpu.VMEM(shape.shape, shape.dtype) for shape in scratch],
        compiler_params=pltpu.CompilerParams(vmem_limit_bytes=min(grant, 62 << 20)),
        cost_estimate=pl.CostEstimate(flops=flops, bytes_accessed=moved, transcendentals=0),
        name=name,
    )(*args)


def array(shape, dtype):
    return jax.ShapeDtypeStruct(shape, dtype)


def paint_kernel(nx, ny, counts, first, split, *refs):
    place = refs[0]
    sources = refs[1 : 1 + len(counts)]
    refs = refs[1 + len(counts) :]
    if not first:
        before, refs = refs[0], refs[2:]
    outs, (rows_ref, a_ref, wh_ref, wl_ref, acc) = refs[:-5], refs[-5:]
    per_z = (TX + 4) * 4
    half = (TZ + 1) * per_z
    total = 0
    for source, count in zip(sources, counts):
        for index in range(count):
            rows_ref[total] = source[pl.ds(8 * index, 8), :]
            total += 1
    x_start, level = place[0], place[1]
    if first:
        acc[...] = jnp.zeros_like(acc)
    else:
        acc[...] = before[...]

    def one_block(index, carry):
        rows = rows_ref[index]
        lanes = rows.shape[1]
        write_y_weights(rows[2:3], ny, wh_ref, wl_ref)
        rel = wrapped_x(rows[1:2], x_start, nx)
        slot = lax.broadcasted_iota(jnp.int32, (16, lanes), 0)
        column = (slot // 4).astype(F32) - rel
        channel = slot % 4
        value = jnp.where(
            channel == 0,
            rows[3:4],
            jnp.where(channel == 1, rows[4:5], jnp.where(channel == 2, rows[5:6], rows[6:7])),
        )
        spread = [value * hat(rows[0:1] - (level + z)) for z in range(TZ + 1)]
        for x in range(0, TX + 4, 4):
            wx = hat(column + float(x))
            for z in range(TZ + 1):
                full = spread[z] * wx
                high = full.astype(BF16)
                row = z * per_z + x * 4
                a_ref[pl.ds(row, 16), :] = high
                a_ref[pl.ds(half + row, 16), :] = (full - high.astype(F32)).astype(BF16)
        dims = (((1,), (1,)), ((), ()))
        main = lax.dot_general(a_ref[...], wh_ref[...], dims, preferred_element_type=F32)
        side = lax.dot_general(
            a_ref[pl.ds(0, half), :], wl_ref[...], dims, preferred_element_type=F32
        )
        acc[...] += main[:half] + main[half:] + side
        return carry

    lax.fori_loop(0, total, one_block, 0)
    if not split:
        outs[0][...] = acc[...]
        return
    sub = TX // 2 * 4
    width = sub + 16
    own = level.astype(jnp.int32) * sub
    for z in range(TZ + 1):
        rows = pl.ds(z * width, width)
        outs[0][rows, :] = acc[pl.ds(pl.multiple_of(z * per_z + own, 16), width), :]
        outs[1][rows, :] = acc[pl.ds(pl.multiple_of(z * per_z + sub - own, 16), width), :]


def paint(place, sources, before, nx, ny, split):
    counts = [source.shape[0] // 8 for source in sources]
    lanes = sources[0].shape[1]
    half = (TZ + 1) * (TX + 4) * 4
    if split:
        shape = array(((TZ + 1) * (TX // 2 + 4) * 4, ny), F32)
        out_shape = (shape, shape)
    else:
        out_shape = array((half, ny), F32)
    return run_kernel(
        functools.partial(paint_kernel, nx, ny, counts, before is None, split),
        "paint",
        [place] + list(sources) + ([] if before is None else list(before)),
        out_shape,
        [
            array((sum(counts), 8, lanes), F32),
            array((2 * half, lanes), BF16),
            array((ny, lanes), BF16),
            array((ny, lanes), BF16),
            array((half, ny), F32),
        ],
        flops=6 * half * lanes * ny * sum(counts),
    )


def prepare_kernel(nz, w1_ref, w2_ref, b1_ref, b2_ref, hw_ref, o1, o2, ob1, ob2, oh, t1, t2):
    rows = 2 * nz * 16
    width = TX // 2
    t1[...] = jnp.zeros_like(t1)
    t2[...] = jnp.zeros_like(t2)

    def at(a, b, e):
        return (a * 3 + b) * 3 + e

    for b in range(3):
        for e in range(3):
            for zo in range(nz):
                first = max(0, 1 - zo)
                last = min(2, nz - zo)
                zi = zo + first - 1
                taps = [w2_ref[at(a, b, e)].astype(F32) for a in range(first, last + 1)]
                strip = jnp.concatenate(taps, axis=1)
                for q in range(2):
                    t2[
                        pl.ds(((e * 2 + q) * nz + zo) * 16, 16),
                        pl.ds(((q + b) * nz + zi) * 16, strip.shape[1]),
                    ] = strip
                for a in range(first, last + 1):
                    for q in range(2):
                        t1[
                            pl.ds(((e * nz + zo + a - 1) * 4 + q + b) * 4, 4),
                            pl.ds((q * nz + zo) * 16, 16),
                        ] = w1_ref[at(a, b, e)].astype(F32)
    o1[...] = t1[...].T.astype(BF16)
    o2[...] = t2[...].astype(BF16)
    cells = nz * width
    lanes = cells * 16
    repeat = (
        lax.broadcasted_iota(jnp.int32, (16, lanes), 0)
        == lax.broadcasted_iota(jnp.int32, (16, lanes), 1) % 16
    )
    tiled = jnp.dot(
        hw_ref[...], jnp.where(repeat, 1.0, 0.0).astype(BF16), preferred_element_type=F32
    )
    row = lax.broadcasted_iota(jnp.int32, (cells, lanes), 0)
    same = (row % width) * nz + row // width == lax.broadcasted_iota(
        jnp.int32, (cells, lanes), 1
    ) // 16
    for k in range(3):
        oh[pl.ds(k * cells, cells), :] = jnp.where(same, tiled[k : k + 1], 0.0).astype(BF16)
    for source, target in ((b1_ref, ob1), (b2_ref, ob2)):
        shape = (rows, 16)
        pick = lax.broadcasted_iota(jnp.int32, shape, 0) % 16 == lax.broadcasted_iota(
            jnp.int32, shape, 1
        )
        column = jnp.sum(
            jnp.where(pick, jnp.broadcast_to(source[...], shape), 0.0), axis=1, keepdims=True
        )
        target[...] = jnp.broadcast_to(column, target.shape)


def prepare(conv1_weight, conv1_bias, conv2_weight, conv2_bias, head_weight, nz):
    w1 = jnp.transpose(conv1_weight, (2, 3, 4, 1, 0)).reshape(27, 4, 16)
    w2 = jnp.transpose(conv2_weight, (2, 3, 4, 0, 1)).reshape(27, 16, 16)
    rows = 2 * nz * 16
    cells = nz * TX // 2
    return run_kernel(
        functools.partial(prepare_kernel, nz),
        "prepare",
        [w1, w2, conv1_bias[None], conv2_bias[None], head_weight],
        (
            array((rows, 3 * nz * 16), BF16),
            array((3 * rows, 4 * nz * 16), BF16),
            array((rows, 128), F32),
            array((rows, 128), F32),
            array((3 * cells, 16 * cells), BF16),
        ),
        [array((3 * nz * 16, rows), F32), array((3 * rows, 4 * nz * 16), F32)],
        flops=1000000,
        smem=0,
    )


def silu(v):
    return v / (1.0 + jnp.exp(-v))


def mesh_kernel(nz, place, keep, got, w1, w2, b1, b2, hw, out, d3, hid, feat):
    per_mid = nz * 16
    rows = 2 * per_mid
    ny = keep.shape[1]
    span = keep.shape[0] // (TZ + 1)
    width = span // 4
    at_low = place[1] == 0.0
    mine, theirs = keep[...], got[...]
    low = jnp.where(at_low, mine, theirs)
    high = jnp.where(at_low, theirs, mine)
    planes = []
    for z in range(nz):
        part = []
        if z <= TZ:
            part.append(low[z * span : (z + 1) * span])
        if z >= nz - TZ - 1:
            index = z - (nz - TZ - 1)
            part.append(high[index * span : (index + 1) * span])
        planes.append(part[0] if len(part) == 1 else part[0] + part[1])
    wide = jnp.concatenate(planes, axis=0).astype(BF16).astype(F32)
    d3[0] = pltpu.roll(wide, 1, 1)
    d3[1] = wide
    d3[2] = pltpu.roll(wide, ny - 1, 1)

    def spread(bias):
        return jnp.concatenate([bias[...]] * (ny // 128), axis=1)

    def hidden(x):
        taps = [
            d3[e, pl.ds(z * span + x * 4, 16), :].astype(BF16)
            for e in range(3)
            for z in range(nz)
        ]
        summed = jnp.dot(w1[...], jnp.concatenate(taps, axis=0), preferred_element_type=F32)
        hid[pl.ds(x * per_mid, rows), :] = silu(summed + spread(b1)).astype(BF16)

    def features(x):
        parts = jnp.dot(
            w2[...], hid[pl.ds(x * per_mid, 2 * rows), :], preferred_element_type=F32
        )
        summed = (
            pltpu.roll(parts[:rows], 1, 1)
            + parts[rows : 2 * rows]
            + pltpu.roll(parts[2 * rows :], ny - 1, 1)
        )
        feat[pl.ds(x * per_mid, rows), :] = silu(summed + spread(b2)).astype(BF16)

    hidden(0)
    hidden(2)
    for x in range(0, width - 4, 2):
        if x + 4 < width - 2:
            hidden(x + 4)
        features(x)
    out[...] = jnp.dot(hw[...], feat[...], preferred_element_type=F32)


def mesh_step(place, keep, got, weights, nz):
    ny = keep.shape[1]
    width = keep.shape[0] // (TZ + 1) // 4
    return run_kernel(
        functools.partial(mesh_kernel, nz),
        "mesh_step",
        [place, keep, got] + list(weights),
        array((3 * nz * (width - 4), ny), F32),
        [
            array((3, nz * width * 4, ny), F32),
            array(((width - 2) * nz * 16, ny), BF16),
            array(((width - 4) * nz * 16, ny), BF16),
        ],
        flops=200000000,
    )


def sample_kernel(nz, nx, ny, count, *refs):
    place, own, other = refs[:3]
    sources, outs = refs[3 : 3 + count], refs[3 + count : 3 + 2 * count]
    f_ref, wh_ref, t_ref = refs[3 + 2 * count :]
    at_low = place[1] == 0.0
    level = place[1].astype(jnp.int32)
    width = TX // 2
    for k in range(3):
        for z in range(TZ + 1):
            rows = pl.ds(pl.multiple_of((k * nz + level + z) * width, width), width)
            mine, theirs = own[rows, :], other[rows, :]
            both = jnp.concatenate(
                [jnp.where(at_low, mine, theirs), jnp.where(at_low, theirs, mine)], axis=0
            )
            f_ref[pl.ds((k * (TZ + 1) + z) * TX, TX), :] = both.astype(BF16)
    x_start = place[0] + 2.0
    for source, out in zip(sources, outs):
        lanes = source.shape[1]
        write_y_weights(source[2:3, :], ny, wh_ref, None)
        t_ref[...] = jnp.dot(f_ref[...], wh_ref[...], preferred_element_type=F32)
        rel = wrapped_x(source[1:2, :], x_start, nx)
        wx = hat(rows_iota(TX, lanes) - rel)
        both = [wx * hat(source[0:1, :] - (place[1] + z)) for z in range(TZ + 1)]
        for k in range(3):
            total = both[0] * t_ref[pl.ds(k * (TZ + 1) * TX, TX), :]
            for z in range(1, TZ + 1):
                total += both[z] * t_ref[pl.ds((k * (TZ + 1) + z) * TX, TX), :]
            out[pl.ds(k, 1), :] = jnp.sum(total, axis=0, keepdims=True)


def sample(place, own, other, sources, nz, nx, ny):
    lanes = sources[0].shape[1]
    cells = 3 * (TZ + 1) * TX
    return run_kernel(
        functools.partial(sample_kernel, nz, nx, ny, len(sources)),
        "sample",
        [place, own, other] + list(sources),
        tuple(array((3, lanes), F32) for _ in sources),
        [array((cells, ny), BF16), array((ny, lanes), BF16), array((cells, lanes), F32)],
        flops=2 * cells * lanes * ny * len(sources),
    )


def finish_kernel(*refs):
    total = refs[0][...]
    for part in refs[1:-1]:
        total += part[...]
    refs[-1][...] = total


def on_device(
    offsets,
    particle_mass,
    velocity,
    home_cell,
    home_tile,
    conv1_weight,
    conv1_bias,
    conv2_weight,
    conv2_bias,
    head_weight,
):
    columns = lax.axis_size("gy")
    rows = lax.axis_size("gx")
    levels = lax.axis_size("gz")
    assert levels == 2
    nz, nx, ny = TZ * levels, TX * rows, TY * columns
    level = lax.axis_index("gz")
    base_z = home_cell // (TX * TY) + level * TZ
    base_x = home_tile // columns * TX + home_cell // TY % TX
    base_y = home_tile % columns * TY + home_cell % TY
    base = jnp.stack([base_z, base_x, base_y]).astype(F32)
    block = jnp.concatenate(
        [
            base + offsets,
            particle_mass[None],
            particle_mass[None] * velocity,
            jnp.zeros_like(particle_mass)[None],
        ],
        axis=0,
    )
    place = jnp.stack([lax.axis_index("gx") * TX - 2, level]).astype(F32)
    line = jnp.concatenate(
        [block]
        + [lax.ppermute(block, "gy", exchange_pairs(columns, s)) for s in range(1, columns)],
        axis=0,
    )
    arrived = [lax.ppermute(line, "gx", exchange_pairs(rows, s)) for s in range(1, rows)]
    weights = prepare(conv1_weight, conv1_bias, conv2_weight, conv2_bias, head_weight, nz)
    early = paint(place, [line], None, nx, ny, False)
    keep, send = paint(place, arrived, (early, weights[2]), nx, ny, True)
    got = lax.ppermute(send, "gz", exchange_pairs(levels, 1))
    own = mesh_step(place, keep, got, weights, nz)
    other = lax.ppermute(own, "gz", exchange_pairs(levels, 1))
    away = sample(place, own, other, arrived, nz, nx, ny)
    home = [
        lax.ppermute(part, "gx", return_pairs(rows, s)) for s, part in enumerate(away, start=1)
    ]
    (here,) = sample(place, own, other, [block], nz, nx, ny)
    return run_kernel(finish_kernel, "finish", [here] + home, here, [], smem=0)


def solution(mesh):
    in_specs = (
        P(None, ("runs", "gx", "gy", "gz")),
        P(("runs", "gx", "gy", "gz")),
        P(None, ("runs", "gx", "gy", "gz")),
        P(("runs", "gx", "gy", "gz")),
        P(("runs", "gx", "gy", "gz")),
        P(),
        P(),
        P(),
        P(),
        P(),
    )
    out_specs = P(None, ("runs", "gx", "gy", "gz"))
    return jax.shard_map(
        on_device, mesh=mesh, in_specs=in_specs, out_specs=out_specs, check_vma=False
    )
```
